32 devices in a mesh: groups: 2 (over x), ctx: 16 (over z, y, core).
Axes of the slice: x: 2, y: 2, z: 4, core: 2. Of those that a mesh axis runs over, the one named last changes fastest.
Arguments:
- q_latent: bfloat16 [128, 1536], P(('groups', 'ctx')), parts along dimension 0, may hold values from -64 to 64
- q_gain: float32 [1536], replicated, may hold values from 0.1 to 1.9
- w_uq: bfloat16 [1536, 24576], P(None, 'ctx'), may hold values from -0.15625 to 0.15625
- w_uk: bfloat16 [128, 128, 512], P('ctx'), may hold values from -0.5 to 0.5
- w_uv: bfloat16 [128, 512, 128], P('ctx'), may hold values from -0.25 to 0.25
- w_o: bfloat16 [16384, 7168], P('ctx'), may hold values from -0.046875 to 0.046875
- latent_cache: bfloat16 [65536, 576], P(('groups', 'ctx')), parts along dimension 0, may hold values from -1024 to 1024
- kv_scales: float32 [65536, 4], P(('groups', 'ctx')), parts along dimension 0, may hold values from 0.5 to 2
- selected: int32 [128, 32], P(('groups', 'ctx')), parts along dimension 0, may hold values from 0 to 511, as said below
- counts: int32 [128], P(('groups', 'ctx')), parts along dimension 0, may hold values from 8 to 32
Outputs:
- attn_out: bfloat16 [128, 7168], P(('groups', 'ctx')), parts along dimension 0
The draws below stay inside these ranges and needn't reach their ends.
There are 2 independent parts, one for each index of `groups`. The reference program is written for one: setup_inputs(seed, part) draws one part's arguments, and reference() takes and returns one part's arrays. A program takes and returns all parts, laid end to end along the dimension named above; an argument that names none is the same for every part. Nothing has to cross between parts.
Inputs may be any that keep to these rules, and one draw needn't show every extreme that they name: `selected`: each row lists 32 different block numbers. Over the rows 4 i to 4 i + 4 - 1 (the query tokens of one device) and their first counts entries, at most 8 different listed blocks lie in the range 32 j to 32 j + 31 for any j.
All inputs are finite; a program needn't handle non-finite values.
Results may differ from the reference program's by a relative error of at most 0.01.
The reference program's roundings to bfloat16 on the way count: a program that leaves them out, or rounds other values in their place, can miss the bound.
Values may be sent and summed in bfloat16 or wider, within the bound.
A program may use at most 128 MiB of HBM per device.

```python
import math
import jax
import jax.numpy as jnp
from jax import lax

QL = 1536
H = 128
DN = 128
DR = 64
DC = 512
DV = 128
D = 7168
TOPB = 32
BLK = 64
NT = 4
Q_DEV = 4
NB_DEV = 32
QTOK = 64
NBLK = 512
CTX = 32768
UB = 64
CAP = 8


def draw_q_latent(key, part):
    seeds = jax.random.split(jax.random.fold_in(key, 11), 4)
    values_all = jnp.clip(jax.random.normal(seeds[0], (QTOK, QL), jnp.float32), -6.0, 6.0)
    row_scale = jnp.exp(jax.random.uniform(seeds[2], (QTOK, 1), jnp.float32, math.log(0.3), math.log(3.0)))
    col_scale = jnp.exp(jax.random.uniform(seeds[3], (1, QL), jnp.float32, math.log(0.3), math.log(3.0)))
    return (values_all * row_scale * col_scale).astype(jnp.bfloat16)


def draw_latent_cache(key, part):
    seeds = jax.random.split(jax.random.fold_in(key, 23), 1)
    values_all = jnp.clip(jax.random.normal(seeds[0], (CTX, DC + DR), jnp.float32), -4.0, 4.0)
    return values_all.astype(jnp.bfloat16)


def routing_tables(key):
    seeds = jax.random.split(jax.random.fold_in(key, 7717), 8)
    n_dev = QTOK // Q_DEV
    pool_size = n_dev * CAP
    hot_owner = jax.random.permutation(seeds[0], n_dev) < 2
    hot_slot = jnp.repeat(hot_owner, CAP)
    priority = jax.random.randint(seeds[1], (n_dev, pool_size), 0, 2 ** 20) + jnp.where(hot_slot, 0, 2 ** 20)[None, :]
    priority = priority * pool_size + jnp.arange(pool_size, dtype=jnp.int32)[None, :]
    chosen = jnp.argsort(priority, axis=1)[:, :UB].astype(jnp.int32)
    local_score = jax.random.randint(seeds[2], (n_dev, n_dev, NB_DEV), 0, 2 ** 20) * NB_DEV + jnp.arange(NB_DEV, dtype=jnp.int32)
    local_pick = jnp.argsort(local_score, axis=2)[:, :, :CAP].astype(jnp.int32).reshape(n_dev, pool_size)
    union_blocks = chosen // CAP * NB_DEV + jnp.take_along_axis(local_pick, chosen, axis=1)
    query_score = jax.random.randint(seeds[3], (n_dev, Q_DEV, UB), 0, 2 ** 20) * UB + jnp.arange(UB, dtype=jnp.int32)
    query_perm = jnp.argsort(query_score, axis=2)[:, :, :TOPB].astype(jnp.int32)
    first_query = jax.random.randint(seeds[5], (n_dev,), 0, Q_DEV)
    query_ids = jnp.arange(Q_DEV, dtype=jnp.int32)[None, :]
    is_first = query_ids == first_query[:, None]
    head_slots = jnp.broadcast_to(jnp.arange(TOPB, dtype=jnp.int32)[None, None, :], (n_dev, Q_DEV, TOPB))
    slot_pick = jnp.where(is_first[:, :, None], head_slots, query_perm)
    spread_union = jnp.broadcast_to(union_blocks[:, None, :], (n_dev, Q_DEV, UB))
    selected = jnp.take_along_axis(spread_union, slot_pick, axis=2)
    fewest = max(1, TOPB // 4)
    live_counts = jax.random.randint(seeds[7], (n_dev, Q_DEV), fewest, TOPB + 1)
    live_counts = jnp.where(is_first, TOPB, live_counts)
    return (selected.reshape(QTOK, TOPB).astype(jnp.int32), live_counts.reshape(QTOK).astype(jnp.int32))


def draw_selected(key, part):
    return routing_tables(key)[0]


def draw_counts(key, part):
    return routing_tables(key)[1]


def block_scale(own_key, dims, cuts, smallest, high):
    def one(axis_at, shards_of):
        draws = jax.random.uniform(jax.random.fold_in(jax.random.fold_in(own_key, 6), axis_at), (shards_of,), jnp.float32, smallest / len(cuts), high / len(cuts))
        return jnp.repeat(jnp.exp(draws), dims[axis_at] // shards_of).reshape((-1,) + (1,) * (len(dims) - axis_at - 1))

    loudness = one(*cuts[0])
    for cut in cuts[1:]:
        loudness = loudness * one(*cut)
    return loudness


def gaussian(own_key, extent, deviation, reach, cuts=(), held_as=jnp.bfloat16):
    drawn = deviation * jax.random.normal(own_key, extent, jnp.float32)
    if cuts:
        drawn = drawn * block_scale(own_key, extent, cuts, -0.22, 0.18)
    return jnp.clip(drawn, -reach, reach).astype(held_as)


def setup_inputs(seed: int = 0, part: int = 0) -> dict:
    streams_of = jax.random.split(jax.random.key(seed), 11)
    own_keys = jax.random.split(jax.random.fold_in(streams_of[10], part), 11)
    q_latent = draw_q_latent(jax.random.fold_in(jax.random.fold_in(streams_of[10], part), 71), part)
    q_gain = jnp.clip(1.0 + 0.18 * jax.random.normal(streams_of[1], (QL,), jnp.float32), 0.1, 1.9)
    w_uq = gaussian(streams_of[2], (QL, H * (DN + DR)), QL ** -0.5, 0.15625, ((1, 16),))
    w_uk = gaussian(streams_of[3], (H, DN, DC), DN ** -0.5, 0.5, ((0, 16),))
    w_uv = gaussian(streams_of[4], (H, DC, DV), DC ** -0.5, 0.25, ((0, 16),))
    w_o = gaussian(streams_of[5], (H * DV, D), (H * DV) ** -0.5, 0.046875, ((0, 16),))
    latent_cache = draw_latent_cache(jax.random.fold_in(jax.random.fold_in(streams_of[10], part), 71), part)
    kv_scales = jnp.clip(jnp.exp(math.log(2.0) - 1.3862944 * jax.random.uniform(own_keys[7], (CTX, NT), jnp.float32) ** block_scale(own_keys[7], (CTX, NT), ((0, 16),), -0.2, 0.2)), 0.5, 2.0)
    selected = draw_selected(jax.random.fold_in(jax.random.fold_in(streams_of[10], part), 71), part)
    counts = draw_counts(jax.random.fold_in(jax.random.fold_in(streams_of[10], part), 71), part)
    return dict(q_latent=q_latent, q_gain=q_gain, w_uq=w_uq, w_uk=w_uk, w_uv=w_uv, w_o=w_o, latent_cache=latent_cache, kv_scales=kv_scales, selected=selected, counts=counts)


norm_eps = 1e-06
rope_base = 10000.0

def rotate_rotary(rotary, positions):
    half_width = rotary.shape[-1] // 2
    freq_index = jnp.arange(half_width, dtype=jnp.float32)
    inverse_freq = jnp.exp(freq_index * (-2.0 * math.log(rope_base) / rotary.shape[-1]))
    angles = positions[:, None] * inverse_freq[None, :]
    cosine = jnp.cos(angles)[:, None, :]
    sine = jnp.sin(angles)[:, None, :]
    first_half = rotary[:, :, :half_width]
    second_half = rotary[:, :, half_width:]
    return jnp.concatenate([first_half * cosine - second_half * sine, first_half * sine + second_half * cosine], axis=2)

def reference(q_latent, q_gain, w_uq, w_uk, w_uv, w_o, latent_cache, kv_scales, selected, counts):
    latent_f = q_latent.astype(jnp.float32)
    normed = (latent_f * lax.rsqrt(lax.optimization_barrier(jnp.mean(latent_f * latent_f, axis=1, keepdims=True)) + norm_eps) * q_gain).astype(jnp.bfloat16)
    projected = jnp.dot(normed, w_uq, preferred_element_type=jnp.float32).reshape(QTOK, H, DN + DR)
    content = projected[:, :, :DN].astype(jnp.bfloat16)
    positions = jnp.arange(QTOK, dtype=jnp.float32)
    rotated = rotate_rotary(projected[:, :, DN:], positions).astype(jnp.bfloat16)
    absorbed = jnp.einsum('qhn,hnc->qhc', content.astype(jnp.float32), w_uk.astype(jnp.float32)).astype(jnp.bfloat16)
    queries = jnp.concatenate([absorbed, rotated], axis=2)
    scaled = (latent_cache[:, :DC].astype(jnp.float32) * jnp.repeat(kv_scales, DC // NT, axis=1)).astype(jnp.bfloat16)
    cache_rows = jnp.concatenate([scaled, latent_cache[:, DC:]], axis=1).reshape(NBLK, BLK, DC + DR)
    softmax_scale = 1.0 / math.sqrt(DN + DR)

    def attend(inputs):
        query_row, blocks, live_count = inputs
        key_rows = cache_rows[blocks].reshape(TOPB * BLK, DC + DR).astype(jnp.float32)
        live_tokens = jnp.repeat(jnp.arange(TOPB, dtype=jnp.int32) < live_count, BLK)
        scores = jnp.dot(query_row.astype(jnp.float32), key_rows.T, preferred_element_type=jnp.float32) * softmax_scale
        scores = jnp.where(live_tokens[None, :], scores, -jnp.inf)
        row_peak = lax.optimization_barrier(jnp.max(scores, axis=1, keepdims=True))
        exponent = jnp.exp(scores - row_peak)
        weights = (exponent / lax.optimization_barrier(jnp.sum(exponent, axis=1, keepdims=True))).astype(jnp.bfloat16)
        return jnp.dot(weights.astype(jnp.float32), key_rows[:, :DC], preferred_element_type=jnp.float32).astype(jnp.bfloat16)
    latent_out = lax.map(attend, (queries, selected, counts))
    head_values = jnp.einsum('qhc,hcv->qhv', latent_out.astype(jnp.float32), w_uv.astype(jnp.float32)).astype(jnp.bfloat16)
    head_values = head_values.reshape(QTOK, H * DV)
    return jnp.dot(head_values, w_o, preferred_element_type=jnp.float32).astype(jnp.bfloat16)
```

```python
import functools
import math

import jax
import jax.numpy as jnp
from jax import lax
from jax.experimental import pallas as pl
from jax.experimental.pallas import tpu as pltpu
from jax.sharding import PartitionSpec as P

BLK = 64
STEP = 4

norm_eps = 1e-06
rope_base = 10000.0
EMPTY = -1e30


def rotate_rotary(rotary, positions):
    half_width = rotary.shape[-1] // 2
    freq_index = jnp.arange(half_width, dtype=jnp.float32)
    inverse_freq = jnp.exp(freq_index * (-2.0 * math.log(rope_base) / rotary.shape[-1]))
    angles = positions[:, None] * inverse_freq[None, :]
    cosine = jnp.cos(angles)[:, None, :]
    sine = jnp.sin(angles)[:, None, :]
    first_half = rotary[:, :, :half_width]
    second_half = rotary[:, :, half_width:]
    return jnp.concatenate(
        [first_half * cosine - second_half * sine, first_half * sine + second_half * cosine], axis=2
    )


def xor_permute(value, n_devices, distance):
    return lax.ppermute(value, "ctx", [(i, i ^ distance) for i in range(n_devices)])


def masks_of(bits):
    out = [0]
    for bit in bits:
        out += [o | bit for o in out]
    return out


def attend_kernel(
    n_parts, n_chunks, width_latent, heads, scale, steps_ref, list_ref, *refs
):
    cache_in = refs[:n_parts]
    q_refs = refs[n_parts : n_parts + n_chunks]
    o_refs = refs[n_parts + n_chunks : n_parts + 2 * n_chunks]
    lse_ref, keys, acc, sems = refs[n_parts + 2 * n_chunks :]
    part_blocks = cache_in[0].shape[0]
    copies = [
        pltpu.make_async_copy(
            cache_in[i], keys.at[pl.ds(i * part_blocks, part_blocks)], sems.at[i]
        )
        for i in range(n_parts)
    ]
    for copy in copies:
        copy.start()
    groups, rows_chunk, _ = q_refs[0].shape
    rows = rows_chunk * n_chunks
    tokens = rows_chunk // heads
    span = STEP * BLK
    token_of_row = (lax.broadcasted_iota(jnp.int32, (rows, 1), 0) // heads) % tokens
    row_bit = lax.shift_left(jnp.ones_like(token_of_row), token_of_row)
    block_of_col = lax.broadcasted_iota(jnp.int32, (1, span), 1) // BLK
    diagonal = lax.broadcasted_iota(jnp.int32, (rows, rows), 0) == lax.broadcasted_iota(
        jnp.int32, (rows, rows), 1
    )
    for copy in copies:
        copy.wait()
    base = 2**tokens

    def group(g, carry):
        query = jnp.concatenate([q[g] for q in q_refs], axis=0)
        acc[...] = jnp.zeros_like(acc)

        def step(s, state):
            peak, total = state
            entries = [list_ref[g, s * STEP + k] for k in range(STEP)]
            key_rows = jnp.concatenate([keys[e // base] for e in entries], axis=0)
            bits = jnp.zeros((1, span), jnp.int32)
            for k in range(STEP):
                bits = jnp.where(block_of_col == k, entries[k] % base, bits)
            live = (bits & row_bit) != 0
            scores = (
                lax.dot_general(
                    query, key_rows, (((1,), (1,)), ((), ())), preferred_element_type=jnp.float32
                )
                * scale
            )
            scores = jnp.where(live, scores, EMPTY)
            new_peak = jnp.maximum(peak, jnp.max(scores, axis=1, keepdims=True))
            fade = jnp.exp(peak - new_peak)
            exponent = jnp.where(live, jnp.exp(scores - new_peak), 0.0)
            acc[...] = acc[...] * fade + jnp.dot(
                exponent.astype(jnp.bfloat16),
                key_rows[:, :width_latent],
                preferred_element_type=jnp.float32,
            )
            return new_peak, total * fade + jnp.sum(exponent, axis=1, keepdims=True)

        peak, total = lax.fori_loop(
            0,
            steps_ref[g],
            step,
            (jnp.full((rows, 1), EMPTY, jnp.float32), jnp.zeros((rows, 1), jnp.float32)),
        )
        some = total > 0.0
        safe = jnp.where(some, total, 1.0)
        out = (acc[...] / safe).astype(jnp.bfloat16)
        for j in range(n_chunks):
            o_refs[j][g] = out[j * rows_chunk : (j + 1) * rows_chunk]
        lse = jnp.where(some, peak + jnp.log(safe), EMPTY)
        lse_ref[pl.ds(g, 1), :] = jnp.sum(
            jnp.where(diagonal, lse, 0.0), axis=0, keepdims=True
        )
        return carry

    lax.fori_loop(0, groups, group, 0)


def attend(parts, chunks, block_list, steps, heads, width_latent, scale):
    n_parts, n_chunks = len(parts), len(chunks)
    part_blocks, _, width_row = parts[0].shape
    groups, rows_chunk, _ = chunks[0].shape
    vmem = pl.BlockSpec(memory_space=pltpu.VMEM)
    smem = pl.BlockSpec(memory_space=pltpu.SMEM)
    out = pl.pallas_call(
        functools.partial(attend_kernel, n_parts, n_chunks, width_latent, heads, scale),
        out_shape=[jax.ShapeDtypeStruct((groups, rows_chunk, width_latent), jnp.bfloat16)] * n_chunks
        + [jax.ShapeDtypeStruct((groups, rows_chunk * n_chunks), jnp.float32)],
        in_specs=[smem, smem] + [pl.BlockSpec(memory_space=pl.ANY)] * n_parts + [vmem] * n_chunks,
        out_specs=[vmem] * (n_chunks + 1),
        scratch_shapes=[
            pltpu.VMEM((n_parts * part_blocks, BLK, width_row), jnp.bfloat16),
            pltpu.VMEM((rows_chunk * n_chunks, width_latent), jnp.float32),
            pltpu.SemaphoreType.DMA((n_parts,)),
        ],
        compiler_params=pltpu.CompilerParams(vmem_limit_bytes=48 * 2**20),
        name="attend",
    )(steps, block_list, *parts, *chunks)
    return out[:n_chunks], out[n_chunks]


def local(
    cache_bits, query_bits, q_latent, q_gain, w_uq, w_uk, w_uv, w_o, latent_cache, kv_scales, selected, counts
):
    n_devices = lax.axis_size("ctx")
    me = lax.axis_index("ctx")
    heads_local, width_content, width_latent = w_uk.shape
    width_row = latent_cache.shape[1]
    width_rotary = width_row - width_latent
    q_local, top_blocks = selected.shape
    blocks_local = latent_cache.shape[0] // BLK
    tiles = kv_scales.shape[1]
    cache_masks, query_masks = masks_of(cache_bits), masks_of(query_bits)
    n_parts = len(cache_masks)

    cache_t = latent_cache.T
    scaled_t = (
        cache_t[:width_latent].astype(jnp.float32).reshape(tiles, width_latent // tiles, -1)
        * kv_scales.T[:, None, :]
    ).astype(jnp.bfloat16)
    own_cache = (
        jnp.concatenate([scaled_t.reshape(width_latent, -1), cache_t[width_latent:]], axis=0)
        .T.reshape(blocks_local, BLK, width_row)
    )
    parts = [own_cache]
    for bit in reversed(cache_bits):
        parts = parts + [xor_permute(p, n_devices, bit) for p in parts]
    parts_masks = [0]
    for bit in reversed(cache_bits):
        parts_masks = parts_masks + [m | bit for m in parts_masks]

    latent_f = q_latent.astype(jnp.float32)
    normed = (
        latent_f
        * lax.rsqrt(jnp.mean(latent_f * latent_f, axis=1, keepdims=True) + norm_eps)
        * q_gain
    ).astype(jnp.bfloat16)
    live_sel = jnp.arange(top_blocks, dtype=jnp.int32)[None, :] < counts[:, None]
    owner = jnp.where(live_sel, selected // blocks_local, -1)
    packed = jnp.concatenate(
        [normed, owner.astype(jnp.bfloat16), (selected % blocks_local).astype(jnp.bfloat16)], axis=1
    )
    gathered = lax.all_gather(packed, "ctx", axis=0, tiled=True)
    row_count = gathered.shape[0]
    latent_width = normed.shape[1]
    all_normed = gathered[:, :latent_width]
    all_owner = gathered[:, latent_width : latent_width + top_blocks].astype(jnp.int32)
    all_inner = gathered[:, latent_width + top_blocks :].astype(jnp.int32)

    projected = jnp.dot(all_normed, w_uq, preferred_element_type=jnp.float32).reshape(
        row_count, heads_local, width_content + width_rotary
    )
    content = projected[:, :, :width_content].astype(jnp.bfloat16)
    positions = jnp.arange(row_count, dtype=jnp.int32).astype(jnp.float32)
    rotated = rotate_rotary(projected[:, :, width_content:], positions).astype(jnp.bfloat16)
    absorbed = jnp.einsum("khn,hnc->khc", content, w_uk, preferred_element_type=jnp.float32).astype(
        jnp.bfloat16
    )
    groups = row_count // q_local
    own_queries = jnp.concatenate([absorbed, rotated], axis=2).reshape(
        groups, q_local * heads_local, width_row
    )
    chunks = [own_queries]
    chunk_masks = [0]
    for bit in reversed(query_bits):
        chunks = chunks + [xor_permute(c, n_devices, bit) for c in chunks]
        chunk_masks = chunk_masks + [m | bit for m in chunk_masks]

    n_held = n_parts * blocks_local
    place = jnp.full_like(all_owner, -1)
    for i, mask in enumerate(parts_masks):
        place = jnp.where(all_owner == (me ^ mask), i * blocks_local + all_inner, place)
    held = jnp.arange(n_held, dtype=jnp.int32)
    member = jnp.any(
        place.reshape(groups, q_local, top_blocks)[:, :, :, None] == held[None, None, None, :], axis=2
    ).astype(jnp.int32)
    bits = jnp.sum(
        member * lax.shift_left(1, jnp.arange(q_local, dtype=jnp.int32))[None, :, None], axis=1
    )
    needed = (bits > 0).astype(jnp.int32)
    rank = jnp.cumsum(needed, axis=1) - needed
    entry = held[None, :] * 2**q_local + bits
    slot = (rank[:, :, None] == held[None, None, :]) & (needed[:, :, None] == 1)
    block_list = jnp.sum(jnp.where(slot, entry[:, :, None], 0), axis=1)
    steps = (jnp.sum(needed, axis=1) + STEP - 1) // STEP

    scale = 1.0 / math.sqrt(width_content + width_rotary)
    outs, lse = attend(parts, chunks, block_list, steps, heads_local, width_latent, scale)

    rows_chunk = q_local * heads_local
    values, logs = [], []
    for i, mask in enumerate(chunk_masks):
        part_lse = lse[:, i * rows_chunk : (i + 1) * rows_chunk]
        values.append(outs[i] if mask == 0 else xor_permute(outs[i], n_devices, mask))
        logs.append(part_lse if mask == 0 else xor_permute(part_lse, n_devices, mask))
    top = functools.reduce(jnp.maximum, logs)
    shares = [jnp.exp(x - top) for x in logs]
    total = functools.reduce(jnp.add, shares)
    latent_out = functools.reduce(
        jnp.add, [v.astype(jnp.float32) * (s / total)[:, :, None] for v, s in zip(values, shares)]
    ).astype(jnp.bfloat16)
    head_out = latent_out.reshape(row_count, heads_local, width_latent)
    head_values = jnp.einsum(
        "qhc,hcv->qhv", head_out, w_uv, preferred_element_type=jnp.float32
    ).astype(jnp.bfloat16)
    head_values = head_values.reshape(row_count, heads_local * w_uv.shape[2])
    result = jnp.dot(head_values, w_o, preferred_element_type=jnp.float32)

    result = result.reshape((2,) * (n_devices.bit_length() - 1) + (q_local, -1))
    axis = n_devices.bit_length() - 2
    bit = 1
    while bit < n_devices:
        mine = (me // bit) % 2
        keep = lax.dynamic_index_in_dim(result, mine, axis, keepdims=False)
        send = lax.dynamic_index_in_dim(result, 1 - mine, axis, keepdims=False)
        result = keep + xor_permute(send.astype(jnp.bfloat16), n_devices, bit).astype(jnp.float32)
        axis -= 1
        bit *= 2
    return result.astype(jnp.bfloat16)


def solution(mesh):
    n_devices = mesh.shape["ctx"]
    all_bits = [1 << i for i in range(n_devices.bit_length() - 1)]
    cache_bits, query_bits = all_bits[:2], all_bits[2:]
    in_specs = (
        P(("groups", "ctx"), None),
        P(),
        P(None, "ctx"),
        P("ctx", None, None),
        P("ctx", None, None),
        P("ctx", None),
        P(("groups", "ctx"), None),
        P(("groups", "ctx"), None),
        P(("groups", "ctx"), None),
        P(("groups", "ctx")),
    )
    out_specs = P(("groups", "ctx"), None)
    return jax.shard_map(
        functools.partial(local, cache_bits, query_bits),
        mesh=mesh,
        in_specs=in_specs,
        out_specs=out_specs,
        check_vma=False,
    )
```

```python
import functools
import math

import jax
import jax.numpy as jnp
from jax import lax
from jax.experimental import pallas as pl
from jax.experimental.pallas import tpu as pltpu
from jax.sharding import PartitionSpec as P

BLK = 64
STEP = 8
SIDE = 2
SPLIT = 1

norm_eps = 1e-06
rope_base = 10000.0
EMPTY = -1e30


def rotate_rotary(rotary, positions):
    half_width = rotary.shape[-1] // 2
    freq_index = jnp.arange(half_width, dtype=jnp.float32)
    inverse_freq = jnp.exp(freq_index * (-2.0 * math.log(rope_base) / rotary.shape[-1]))
    angles = positions[:, None] * inverse_freq[None, :]
    cosine = jnp.cos(angles)[:, None, :]
    sine = jnp.sin(angles)[:, None, :]
    first_half = rotary[:, :, :half_width]
    second_half = rotary[:, :, half_width:]
    return jnp.concatenate(
        [first_half * cosine - second_half * sine, first_half * sine + second_half * cosine], axis=2
    )


def xor_permute(value, n_devices, distance):
    return lax.ppermute(value, "ctx", [(i, i ^ distance) for i in range(n_devices)])


def masks_of(bits):
    out = [0]
    for bit in bits:
        out += [o | bit for o in out]
    return out


def gather_kernel(n_devices, own_ref, out_ref, send_sems, recv_sems):
    me = lax.axis_index("ctx")
    barrier = pltpu.get_barrier_semaphore()
    for d in range(1, n_devices):
        pl.semaphore_signal(barrier, inc=1, device_id={"ctx": (me + d) % n_devices})
    pl.semaphore_wait(barrier, n_devices - 1)
    copies = [
        pltpu.make_async_remote_copy(
            src_ref=own_ref,
            dst_ref=out_ref.at[me],
            send_sem=send_sems.at[d],
            recv_sem=recv_sems.at[d],
            device_id={"ctx": (me + d) % n_devices},
        )
        for d in range(1, n_devices)
    ]
    for copy in copies:
        copy.start()
    out_ref[me] = own_ref[...]
    for copy in copies:
        copy.wait()


def gather_rows(own, n_devices):
    vmem = pl.BlockSpec(memory_space=pltpu.VMEM)
    out = pl.pallas_call(
        functools.partial(gather_kernel, n_devices),
        out_shape=jax.ShapeDtypeStruct((n_devices,) + own.shape, own.dtype),
        in_specs=[vmem],
        out_specs=vmem,
        scratch_shapes=[pltpu.SemaphoreType.DMA((n_devices,)), pltpu.SemaphoreType.DMA((n_devices,))],
        compiler_params=pltpu.CompilerParams(collective_id=0, has_side_effects=True),
        name="gather_rows",
    )(own)
    return out.reshape(n_devices * own.shape[0], own.shape[1])


def attend_kernel(
    n_parts, n_chunks, first, width_latent, heads, scale, steps_ref, list_ref, *refs
):
    cache_in = refs[:n_parts]
    q_refs = refs[n_parts : n_parts + n_chunks]
    o_refs = refs[n_parts + n_chunks : n_parts + 2 * n_chunks]
    lse_ref, keys, acc, sems = refs[n_parts + 2 * n_chunks :]
    part_blocks = cache_in[0].shape[0]
    copies = [
        pltpu.make_async_copy(
            cache_in[i], keys.at[pl.ds(i * part_blocks, part_blocks)], sems.at[i]
        )
        for i in range(n_parts)
    ]
    for copy in copies:
        copy.start()
    groups, rows_chunk, _ = o_refs[0].shape
    rows = rows_chunk * n_chunks
    tokens = rows_chunk // heads
    span = STEP * BLK
    token_of_row = (lax.broadcasted_iota(jnp.int32, (rows, 1), 0) // heads) % tokens
    row_bit = lax.shift_left(jnp.ones_like(token_of_row), token_of_row)
    block_of_col = lax.broadcasted_iota(jnp.int32, (1, span), 1) // BLK
    diagonal = lax.broadcasted_iota(jnp.int32, (rows, rows), 0) == lax.broadcasted_iota(
        jnp.int32, (rows, rows), 1
    )
    for copy in copies:
        copy.wait()
    base = 2**tokens

    def one_step(i, g, query, s, peak, total):
        entries = [list_ref[g, s * STEP + k] for k in range(STEP)]
        key_rows = jnp.concatenate([keys[e // base] for e in entries], axis=0)
        bits = jnp.zeros((1, span), jnp.int32)
        for k in range(STEP):
            bits = jnp.where(block_of_col == k, entries[k] % base, bits)
        live = (bits & row_bit) != 0
        scores = (
            lax.dot_general(
                query, key_rows, (((1,), (1,)), ((), ())), preferred_element_type=jnp.float32
            )
            * scale
        )
        scores = jnp.where(live, scores, EMPTY)
        new_peak = jnp.maximum(peak, jnp.max(scores, axis=1, keepdims=True))
        fade = jnp.exp(peak - new_peak)
        exponent = jnp.where(live, jnp.exp(scores - new_peak), 0.0)
        acc[i] = acc[i] * fade + jnp.dot(
            exponent.astype(jnp.bfloat16),
            key_rows[:, :width_latent],
            preferred_element_type=jnp.float32,
        )
        return new_peak, total * fade + jnp.sum(exponent, axis=1, keepdims=True)

    def some_groups(block, carry):
        local_g = [block * SIDE + i for i in range(SIDE)]
        g = [first + x for x in local_g]
        query = [jnp.concatenate([q[x] for q in q_refs], axis=0) for x in g]
        acc[...] = jnp.zeros_like(acc)

        def step(s, states):
            return tuple(
                one_step(i, g[i], query[i], s, *states[i]) for i in range(SIDE)
            )

        start = (jnp.full((rows, 1), EMPTY, jnp.float32), jnp.zeros((rows, 1), jnp.float32))
        n_steps = functools.reduce(jnp.maximum, [steps_ref[x] for x in g])
        states = lax.fori_loop(0, n_steps, step, (start,) * SIDE)
        for i in range(SIDE):
            peak, total = states[i]
            some = total > 0.0
            safe = jnp.where(some, total, 1.0)
            out = (acc[i] / safe).astype(jnp.bfloat16)
            for j in range(n_chunks):
                o_refs[j][local_g[i]] = out[j * rows_chunk : (j + 1) * rows_chunk]
            lse = jnp.where(some, peak + jnp.log(safe), EMPTY)
            lse_ref[pl.ds(local_g[i], 1), :] = jnp.sum(
                jnp.where(diagonal, lse, 0.0), axis=0, keepdims=True
            )
        return carry

    lax.fori_loop(0, groups // SIDE, some_groups, 0)


def attend(parts, chunks, block_list, steps, first, groups, heads, width_latent, scale):
    n_parts, n_chunks = len(parts), len(chunks)
    part_blocks, _, width_row = parts[0].shape
    rows_chunk = chunks[0].shape[1]
    vmem = pl.BlockSpec(memory_space=pltpu.VMEM)
    smem = pl.BlockSpec(memory_space=pltpu.SMEM)
    out = pl.pallas_call(
        functools.partial(attend_kernel, n_parts, n_chunks, first, width_latent, heads, scale),
        out_shape=[jax.ShapeDtypeStruct((groups, rows_chunk, width_latent), jnp.bfloat16)] * n_chunks
        + [jax.ShapeDtypeStruct((groups, rows_chunk * n_chunks), jnp.float32)],
        in_specs=[smem, smem] + [pl.BlockSpec(memory_space=pl.ANY)] * n_parts + [vmem] * n_chunks,
        out_specs=[vmem] * (n_chunks + 1),
        scratch_shapes=[
            pltpu.VMEM((n_parts * part_blocks, BLK, width_row), jnp.bfloat16),
            pltpu.VMEM((SIDE, rows_chunk * n_chunks, width_latent), jnp.float32),
            pltpu.SemaphoreType.DMA((n_parts,)),
        ],
        compiler_params=pltpu.CompilerParams(vmem_limit_bytes=48 * 2**20),
        name="attend",
        cost_estimate=pl.CostEstimate(
            flops=2 * groups * rows_chunk * n_chunks * part_blocks * BLK * (width_row + width_latent),
            bytes_accessed=2 * n_parts * part_blocks * BLK * width_row,
            transcendentals=0,
        ),
    )(steps, block_list, *parts, *chunks)
    return out[:n_chunks], out[n_chunks]


def combine(partials):
    if len(partials) == 1:
        return partials[0]
    logs = [log for _, log in partials]
    top = functools.reduce(jnp.maximum, logs)
    shares = [jnp.exp(x - top) for x in logs]
    total = functools.reduce(jnp.add, shares)
    value = functools.reduce(
        jnp.add,
        [v.astype(jnp.float32) * (s / total)[:, :, None] for (v, _), s in zip(partials, shares)],
    ).astype(jnp.bfloat16)
    return value, top + jnp.log(total)


def local(
    cache_bits, query_bits, q_latent, q_gain, w_uq, w_uk, w_uv, w_o, latent_cache, kv_scales, selected, counts
):
    n_devices = lax.axis_size("ctx")
    me = lax.axis_index("ctx")
    heads_local, width_content, width_latent = w_uk.shape
    width_row = latent_cache.shape[1]
    width_rotary = width_row - width_latent
    q_local, top_blocks = selected.shape
    blocks_local = latent_cache.shape[0] // BLK
    tiles = kv_scales.shape[1]
    cache_masks, query_masks = masks_of(cache_bits), masks_of(query_bits)
    n_parts = len(cache_masks)

    cache_t = latent_cache.T
    scaled_t = (
        cache_t[:width_latent].astype(jnp.float32).reshape(tiles, width_latent // tiles, -1)
        * kv_scales.T[:, None, :]
    ).astype(jnp.bfloat16)
    own_cache = (
        jnp.concatenate([scaled_t.reshape(width_latent, -1), cache_t[width_latent:]], axis=0)
        .T.reshape(blocks_local, BLK, width_row)
    )
    latent_f = q_latent.astype(jnp.float32)
    normed = (
        latent_f
        * lax.rsqrt(jnp.mean(latent_f * latent_f, axis=1, keepdims=True) + norm_eps)
        * q_gain
    ).astype(jnp.bfloat16)
    live_sel = jnp.arange(top_blocks, dtype=jnp.int32)[None, :] < counts[:, None]
    owner = jnp.where(live_sel, selected // blocks_local, -1)
    row_width = normed.shape[1] + 2 * top_blocks
    packed = jnp.concatenate(
        [
            normed,
            owner.astype(jnp.bfloat16),
            (selected % blocks_local).astype(jnp.bfloat16),
            jnp.zeros((q_local, -row_width % 128), jnp.bfloat16),
        ],
        axis=1,
    )
    gathered = gather_rows(packed, n_devices)
    gathered, own_cache = lax.optimization_barrier((gathered, own_cache))
    parts = [own_cache]
    for bit in reversed(cache_bits):
        parts = parts + [xor_permute(p, n_devices, bit) for p in parts]
    parts_masks = [0]
    for bit in reversed(cache_bits):
        parts_masks = parts_masks + [m | bit for m in parts_masks]

    row_count = gathered.shape[0]
    latent_width = normed.shape[1]
    all_normed = gathered[:, :latent_width]
    all_owner = gathered[:, latent_width : latent_width + top_blocks].astype(jnp.int32)
    all_inner = gathered[:, latent_width + top_blocks : row_width].astype(jnp.int32)

    projected = jnp.dot(all_normed, w_uq, preferred_element_type=jnp.float32).reshape(
        row_count, heads_local, width_content + width_rotary
    )
    content = projected[:, :, :width_content].astype(jnp.bfloat16)
    positions = jnp.arange(row_count, dtype=jnp.int32).astype(jnp.float32)
    rotated = rotate_rotary(projected[:, :, width_content:], positions).astype(jnp.bfloat16)
    absorbed = jnp.einsum("khn,hnc->khc", content, w_uk, preferred_element_type=jnp.float32).astype(
        jnp.bfloat16
    )
    groups = row_count // q_local
    own_queries = jnp.concatenate([absorbed, rotated], axis=2).reshape(
        groups, q_local * heads_local, width_row
    )
    chunks = [own_queries]
    chunk_masks = [0]
    for bit in reversed(query_bits):
        chunks = chunks + [xor_permute(c, n_devices, bit) for c in chunks]
        chunk_masks = chunk_masks + [m | bit for m in chunk_masks]

    n_held = n_parts * blocks_local
    place = jnp.full_like(all_owner, -1)
    for i, mask in enumerate(parts_masks):
        place = jnp.where(all_owner == (me ^ mask), i * blocks_local + all_inner, place)
    held = jnp.arange(n_held, dtype=jnp.int32)
    member = jnp.any(
        place.reshape(groups, q_local, top_blocks)[:, :, :, None] == held[None, None, None, :], axis=2
    ).astype(jnp.int32)
    bits = jnp.sum(
        member * lax.shift_left(1, jnp.arange(q_local, dtype=jnp.int32))[None, :, None], axis=1
    )
    needed = (bits > 0).astype(jnp.int32)
    rank = jnp.cumsum(needed, axis=1) - needed
    entry = held[None, :] * 2**q_local + bits
    slot = (rank[:, :, None] == held[None, None, :]) & (needed[:, :, None] == 1)
    block_list = jnp.sum(jnp.where(slot, entry[:, :, None], 0), axis=1)
    steps = (jnp.sum(needed, axis=1) + STEP - 1) // STEP

    scale = 1.0 / math.sqrt(width_content + width_rotary)
    rows_chunk = q_local * heads_local
    groups_call = groups // SPLIT
    halves = []
    for first in range(0, groups, groups_call):
        outs, lse = attend(
            parts, chunks, block_list, steps, first, groups_call, heads_local, width_latent, scale
        )
        held_for = {
            mask: [(outs[i], lse[:, i * rows_chunk : (i + 1) * rows_chunk])]
            for i, mask in enumerate(chunk_masks)
        }
        for bit in query_bits:
            leaving = sorted([m for m in held_for if m & bit], reverse=True)
            going = [combine(held_for.pop(m)) for m in leaving]
            logs = xor_permute(jnp.stack([log for _, log in going]), n_devices, bit)
            for i, mask in enumerate(leaving):
                value = xor_permute(going[i][0], n_devices, bit)
                held_for[mask ^ bit].append((value, logs[i]))
        halves.append(combine(held_for[0])[0])
    latent_out = jnp.concatenate(halves, axis=0)
    head_out = latent_out.reshape(row_count, heads_local, width_latent)
    head_values = jnp.einsum(
        "qhc,hcv->qhv", head_out, w_uv, preferred_element_type=jnp.float32
    ).astype(jnp.bfloat16)
    head_values = head_values.reshape(row_count, heads_local * w_uv.shape[2])
    result = jnp.dot(head_values, w_o, preferred_element_type=jnp.float32)

    result = result.reshape((2,) * (n_devices.bit_length() - 1) + (q_local, -1))
    axis = n_devices.bit_length() - 2
    bit = 1
    while bit < n_devices:
        mine = (me // bit) % 2
        keep = lax.dynamic_index_in_dim(result, mine, axis, keepdims=False)
        send = lax.dynamic_index_in_dim(result, 1 - mine, axis, keepdims=False)
        result = keep + xor_permute(send.astype(jnp.bfloat16), n_devices, bit).astype(jnp.float32)
        axis -= 1
        bit *= 2
    return result.astype(jnp.bfloat16)


def solution(mesh):
    n_devices = mesh.shape["ctx"]
    all_bits = [1 << i for i in range(n_devices.bit_length() - 1)]
    cache_bits, query_bits = all_bits[:2], all_bits[2:]
    in_specs = (
        P(("groups", "ctx"), None),
        P(),
        P(None, "ctx"),
        P("ctx", None, None),
        P("ctx", None, None),
        P("ctx", None),
        P(("groups", "ctx"), None),
        P(("groups", "ctx"), None),
        P(("groups", "ctx"), None),
        P(("groups", "ctx")),
    )
    out_specs = P(("groups", "ctx"), None)
    return jax.shard_map(
        functools.partial(local, cache_bits, query_bits),
        mesh=mesh,
        in_specs=in_specs,
        out_specs=out_specs,
        check_vma=False,
    )
```

```python
import functools
import math

import jax
import jax.numpy as jnp
from jax import lax
from jax.experimental import pallas as pl
from jax.experimental.pallas import tpu as pltpu
from jax.sharding import PartitionSpec as P

BLK = 64
STEP = 8
SIDE = 2
SPLIT = 1

norm_eps = 1e-06
rope_base = 10000.0
EMPTY = -1e30


def rotate_rotary(rotary, positions):
    half_width = rotary.shape[-1] // 2
    freq_index = jnp.arange(half_width, dtype=jnp.float32)
    inverse_freq = jnp.exp(freq_index * (-2.0 * math.log(rope_base) / rotary.shape[-1]))
    angles = positions[:, None] * inverse_freq[None, :]
    cosine = jnp.cos(angles)[:, None, :]
    sine = jnp.sin(angles)[:, None, :]
    first_half = rotary[:, :, :half_width]
    second_half = rotary[:, :, half_width:]
    return jnp.concatenate(
        [first_half * cosine - second_half * sine, first_half * sine + second_half * cosine], axis=2
    )


def xor_permute(value, n_devices, distance):
    return lax.ppermute(value, "ctx", [(i, i ^ distance) for i in range(n_devices)])


def gather_kernel(n_devices, own_ref, out_ref, send_sems, recv_sems):
    me = lax.axis_index("ctx")
    barrier = pltpu.get_barrier_semaphore()
    for d in range(1, n_devices):
        pl.semaphore_signal(barrier, inc=1, device_id={"ctx": (me + d) % n_devices})
    pl.semaphore_wait(barrier, n_devices - 1)
    copies = [
        pltpu.make_async_remote_copy(
            src_ref=own_ref,
            dst_ref=out_ref.at[me],
            send_sem=send_sems.at[d],
            recv_sem=recv_sems.at[d],
            device_id={"ctx": (me + d) % n_devices},
        )
        for d in range(1, n_devices)
    ]
    for copy in copies:
        copy.start()
    out_ref[me] = own_ref[...]
    for copy in copies:
        copy.wait()


def gather_rows(own, n_devices):
    vmem = pl.BlockSpec(memory_space=pltpu.VMEM)
    out = pl.pallas_call(
        functools.partial(gather_kernel, n_devices),
        out_shape=jax.ShapeDtypeStruct((n_devices,) + own.shape, own.dtype),
        in_specs=[vmem],
        out_specs=vmem,
        scratch_shapes=[pltpu.SemaphoreType.DMA((n_devices,)), pltpu.SemaphoreType.DMA((n_devices,))],
        compiler_params=pltpu.CompilerParams(collective_id=0, has_side_effects=True),
        name="gather_rows",
    )(own)
    return out.reshape(n_devices * own.shape[0], own.shape[1])


def attend_kernel(
    n_parts, n_chunks, first, width_latent, heads, scale, steps_ref, list_ref, *refs
):
    cache_in = refs[:n_parts]
    q_refs = refs[n_parts : n_parts + n_chunks]
    o_refs = refs[n_parts + n_chunks : n_parts + 2 * n_chunks]
    lse_ref, keys, acc, sems = refs[n_parts + 2 * n_chunks :]
    part_blocks = cache_in[0].shape[0]
    copies = [
        pltpu.make_async_copy(
            cache_in[i], keys.at[pl.ds(i * part_blocks, part_blocks)], sems.at[i]
        )
        for i in range(n_parts)
    ]
    for copy in copies:
        copy.start()
    groups, rows_chunk, _ = o_refs[0].shape
    rows = rows_chunk * n_chunks
    tokens = rows_chunk // heads
    span = STEP * BLK
    token_of_row = (lax.broadcasted_iota(jnp.int32, (rows, 1), 0) // heads) % tokens
    row_bit = lax.shift_left(jnp.ones_like(token_of_row), token_of_row)
    block_of_col = lax.broadcasted_iota(jnp.int32, (1, span), 1) // BLK
    diagonal = lax.broadcasted_iota(jnp.int32, (rows, rows), 0) == lax.broadcasted_iota(
        jnp.int32, (rows, rows), 1
    )
    for copy in copies:
        copy.wait()
    base = 2**tokens

    def one_step(i, g, query, s, peak, total):
        entries = [list_ref[g, s * STEP + k] for k in range(STEP)]
        key_rows = jnp.concatenate([keys[e // base] for e in entries], axis=0)
        bits = jnp.zeros((1, span), jnp.int32)
        for k in range(STEP):
            bits = jnp.where(block_of_col == k, entries[k] % base, bits)
        live = (bits & row_bit) != 0
        scores = (
            lax.dot_general(
                query, key_rows, (((1,), (1,)), ((), ())), preferred_element_type=jnp.float32
            )
            * scale
        )
        scores = jnp.where(live, scores, EMPTY)
        new_peak = jnp.maximum(peak, jnp.max(scores, axis=1, keepdims=True))
        fade = jnp.exp(peak - new_peak)
        exponent = jnp.where(live, jnp.exp(scores - new_peak), 0.0)
        acc[i] = acc[i] * fade + jnp.dot(
            exponent.astype(jnp.bfloat16),
            key_rows[:, :width_latent],
            preferred_element_type=jnp.float32,
        )
        return new_peak, total * fade + jnp.sum(exponent, axis=1, keepdims=True)

    def some_groups(block, carry):
        local_g = [block * SIDE + i for i in range(SIDE)]
        g = [first + x for x in local_g]
        query = [jnp.concatenate([q[x] for q in q_refs], axis=0) for x in g]
        acc[...] = jnp.zeros_like(acc)

        def step(s, states):
            return tuple(
                one_step(i, g[i], query[i], s, *states[i]) for i in range(SIDE)
            )

        start = (jnp.full((rows, 1), EMPTY, jnp.float32), jnp.zeros((rows, 1), jnp.float32))
        n_steps = functools.reduce(jnp.maximum, [steps_ref[x] for x in g])
        states = lax.fori_loop(0, n_steps, step, (start,) * SIDE)
        for i in range(SIDE):
            peak, total = states[i]
            some = total > 0.0
            safe = jnp.where(some, total, 1.0)
            out = (acc[i] / safe).astype(jnp.bfloat16)
            for j in range(n_chunks):
                o_refs[j][local_g[i]] = out[j * rows_chunk : (j + 1) * rows_chunk]
            lse = jnp.where(some, peak + jnp.log(safe), EMPTY)
            lse_ref[pl.ds(local_g[i], 1), :] = jnp.sum(
                jnp.where(diagonal, lse, 0.0), axis=0, keepdims=True
            )
        return carry

    lax.fori_loop(0, groups // SIDE, some_groups, 0)


def attend(parts, chunks, block_list, steps, first, groups, heads, width_latent, scale):
    n_parts, n_chunks = len(parts), len(chunks)
    part_blocks, _, width_row = parts[0].shape
    rows_chunk = chunks[0].shape[1]
    vmem = pl.BlockSpec(memory_space=pltpu.VMEM)
    smem = pl.BlockSpec(memory_space=pltpu.SMEM)
    out = pl.pallas_call(
        functools.partial(attend_kernel, n_parts, n_chunks, first, width_latent, heads, scale),
        out_shape=[jax.ShapeDtypeStruct((groups, rows_chunk, width_latent), jnp.bfloat16)] * n_chunks
        + [jax.ShapeDtypeStruct((groups, rows_chunk * n_chunks), jnp.float32)],
        in_specs=[smem, smem] + [pl.BlockSpec(memory_space=pl.ANY)] * n_parts + [vmem] * n_chunks,
        out_specs=[vmem] * (n_chunks + 1),
        scratch_shapes=[
            pltpu.VMEM((n_parts * part_blocks, BLK, width_row), jnp.bfloat16),
            pltpu.VMEM((SIDE, rows_chunk * n_chunks, width_latent), jnp.float32),
            pltpu.SemaphoreType.DMA((n_parts,)),
        ],
        compiler_params=pltpu.CompilerParams(vmem_limit_bytes=48 * 2**20),
        name="attend",
        cost_estimate=pl.CostEstimate(
            flops=2 * groups * rows_chunk * n_chunks * part_blocks * BLK * (width_row + width_latent),
            bytes_accessed=2 * n_parts * part_blocks * BLK * width_row,
            transcendentals=0,
        ),
    )(steps, block_list, *parts, *chunks)
    return out[:n_chunks], out[n_chunks]


def combine(partials):
    if len(partials) == 1:
        return partials[0]
    logs = [log for _, log in partials]
    top = functools.reduce(jnp.maximum, logs)
    shares = [jnp.exp(x - top) for x in logs]
    total = functools.reduce(jnp.add, shares)
    value = functools.reduce(
        jnp.add,
        [v.astype(jnp.float32) * (s / total)[:, :, None] for (v, _), s in zip(partials, shares)],
    ).astype(jnp.bfloat16)
    return value, top + jnp.log(total)


def local(
    cache_bits, query_bits, q_latent, q_gain, w_uq, w_uk, w_uv, w_o, latent_cache, kv_scales, selected, counts
):
    n_devices = lax.axis_size("ctx")
    me = lax.axis_index("ctx")
    heads_local, width_content, width_latent = w_uk.shape
    width_row = latent_cache.shape[1]
    width_rotary = width_row - width_latent
    q_local, top_blocks = selected.shape
    blocks_local = latent_cache.shape[0] // BLK
    tiles = kv_scales.shape[1]
    n_parts = 2 ** len(cache_bits)

    cache_t = latent_cache.T
    scaled_t = (
        cache_t[:width_latent].astype(jnp.float32).reshape(tiles, width_latent // tiles, -1)
        * kv_scales.T[:, None, :]
    ).astype(jnp.bfloat16)
    own_cache = (
        jnp.concatenate([scaled_t.reshape(width_latent, -1), cache_t[width_latent:]], axis=0)
        .T.reshape(blocks_local, BLK, width_row)
    )
    latent_f = q_latent.astype(jnp.float32)
    normed = (
        latent_f
        * lax.rsqrt(jnp.mean(latent_f * latent_f, axis=1, keepdims=True) + norm_eps)
        * q_gain
    ).astype(jnp.bfloat16)
    live_sel = jnp.arange(top_blocks, dtype=jnp.int32)[None, :] < counts[:, None]
    owner = jnp.where(live_sel, selected // blocks_local, -1)
    row_width = normed.shape[1] + 2 * top_blocks
    packed = jnp.concatenate(
        [
            normed,
            owner.astype(jnp.bfloat16),
            (selected % blocks_local).astype(jnp.bfloat16),
            jnp.zeros((q_local, -row_width % 128), jnp.bfloat16),
        ],
        axis=1,
    )
    gathered = gather_rows(packed, n_devices)
    gathered, own_cache = lax.optimization_barrier((gathered, own_cache))
    near_bit, far_bit = cache_bits
    far = xor_permute(own_cache, n_devices, far_bit)
    near = xor_permute(own_cache, n_devices, near_bit)
    parts_masks = [0, far_bit, near_bit, far_bit | near_bit]
    row_count = gathered.shape[0]
    latent_width = normed.shape[1]
    all_normed = gathered[:, :latent_width]
    all_owner = gathered[:, latent_width : latent_width + top_blocks].astype(jnp.int32)
    all_inner = gathered[:, latent_width + top_blocks : row_width].astype(jnp.int32)

    projected = jnp.dot(all_normed, w_uq, preferred_element_type=jnp.float32).reshape(
        row_count, heads_local, width_content + width_rotary
    )
    content = projected[:, :, :width_content].astype(jnp.bfloat16)
    positions = jnp.arange(row_count, dtype=jnp.int32).astype(jnp.float32)
    rotated = rotate_rotary(projected[:, :, width_content:], positions).astype(jnp.bfloat16)
    absorbed = jnp.einsum("khn,hnc->khc", content, w_uk, preferred_element_type=jnp.float32).astype(
        jnp.bfloat16
    )
    groups = row_count // q_local
    own_queries = jnp.concatenate([absorbed, rotated], axis=2).reshape(
        groups, q_local * heads_local, width_row
    )
    chunks = [own_queries]
    chunk_masks = [0]
    for bit in reversed(query_bits):
        chunks = chunks + [xor_permute(c, n_devices, bit) for c in chunks]
        chunk_masks = chunk_masks + [m | bit for m in chunk_masks]

    far, chunks[-1] = lax.optimization_barrier((far, chunks[-1]))
    parts = [own_cache, far, near, xor_permute(far, n_devices, near_bit)]

    n_held = n_parts * blocks_local
    place = jnp.full_like(all_owner, -1)
    for i, mask in enumerate(parts_masks):
        place = jnp.where(all_owner == (me ^ mask), i * blocks_local + all_inner, place)
    held = jnp.arange(n_held, dtype=jnp.int32)
    member = jnp.any(
        place.reshape(groups, q_local, top_blocks)[:, :, :, None] == held[None, None, None, :], axis=2
    ).astype(jnp.int32)
    bits = jnp.sum(
        member * lax.shift_left(1, jnp.arange(q_local, dtype=jnp.int32))[None, :, None], axis=1
    )
    needed = (bits > 0).astype(jnp.int32)
    rank = jnp.cumsum(needed, axis=1) - needed
    entry = held[None, :] * 2**q_local + bits
    slot = (rank[:, :, None] == held[None, None, :]) & (needed[:, :, None] == 1)
    block_list = jnp.sum(jnp.where(slot, entry[:, :, None], 0), axis=1)
    steps = (jnp.sum(needed, axis=1) + STEP - 1) // STEP

    scale = 1.0 / math.sqrt(width_content + width_rotary)
    rows_chunk = q_local * heads_local
    groups_call = groups // SPLIT
    halves = []
    for first in range(0, groups, groups_call):
        outs, lse = attend(
            parts, chunks, block_list, steps, first, groups_call, heads_local, width_latent, scale
        )
        held_for = {
            mask: [(outs[i], lse[:, i * rows_chunk : (i + 1) * rows_chunk])]
            for i, mask in enumerate(chunk_masks)
        }
        for bit in query_bits:
            leaving = sorted([m for m in held_for if m & bit], reverse=True)
            going = [combine(held_for.pop(m)) for m in leaving]
            logs = xor_permute(jnp.stack([log for _, log in going]), n_devices, bit)
            for i, mask in enumerate(leaving):
                value = xor_permute(going[i][0], n_devices, bit)
                held_for[mask ^ bit].append((value, logs[i]))
        halves.append(combine(held_for[0])[0])
    latent_out = jnp.concatenate(halves, axis=0)
    head_out = latent_out.reshape(row_count, heads_local, width_latent)
    head_values = jnp.einsum(
        "qhc,hcv->qhv", head_out, w_uv, preferred_element_type=jnp.float32
    ).astype(jnp.bfloat16)
    head_values = head_values.reshape(row_count, heads_local * w_uv.shape[2])
    result = jnp.dot(head_values, w_o, preferred_element_type=jnp.float32)

    result = result.reshape((2,) * (n_devices.bit_length() - 1) + (q_local, -1))
    axis = n_devices.bit_length() - 2
    bit = 1
    while bit < n_devices:
        mine = (me // bit) % 2
        keep = lax.dynamic_index_in_dim(result, mine, axis, keepdims=False)
        send = lax.dynamic_index_in_dim(result, 1 - mine, axis, keepdims=False)
        result = keep + xor_permute(send.astype(jnp.bfloat16), n_devices, bit).astype(jnp.float32)
        axis -= 1
        bit *= 2
    return result.astype(jnp.bfloat16)


def solution(mesh):
    n_devices = mesh.shape["ctx"]
    all_bits = [1 << i for i in range(n_devices.bit_length() - 1)]
    cache_bits, query_bits = all_bits[:2], all_bits[2:]
    in_specs = (
        P(("groups", "ctx"), None),
        P(),
        P(None, "ctx"),
        P("ctx", None, None),
        P("ctx", None, None),
        P("ctx", None),
        P(("groups", "ctx"), None),
        P(("groups", "ctx"), None),
        P(("groups", "ctx"), None),
        P(("groups", "ctx")),
    )
    out_specs = P(("groups", "ctx"), None)
    return jax.shard_map(
        functools.partial(local, cache_bits, query_bits),
        mesh=mesh,
        in_specs=in_specs,
        out_specs=out_specs,
        check_vma=False,
    )
```

```python
import functools
import math

import jax
import jax.numpy as jnp
from jax import lax
from jax.experimental import pallas as pl
from jax.experimental.pallas import tpu as pltpu
from jax.sharding import PartitionSpec as P

BLK = 64
STEP = 8
SIDE = 2
TILES = 7
SPLIT = 1

norm_eps = 1e-06
rope_base = 10000.0
EMPTY = -1e30


def rotate_rotary(rotary, positions):
    half_width = rotary.shape[-1] // 2
    freq_index = jnp.arange(half_width, dtype=jnp.float32)
    inverse_freq = jnp.exp(freq_index * (-2.0 * math.log(rope_base) / rotary.shape[-1]))
    angles = positions[:, None] * inverse_freq[None, :]
    cosine = jnp.cos(angles)[:, None, :]
    sine = jnp.sin(angles)[:, None, :]
    first_half = rotary[:, :, :half_width]
    second_half = rotary[:, :, half_width:]
    return jnp.concatenate(
        [first_half * cosine - second_half * sine, first_half * sine + second_half * cosine], axis=2
    )


def xor_permute(value, n_devices, distance):
    return lax.ppermute(value, "ctx", [(i, i ^ distance) for i in range(n_devices)])


def gather_kernel(n_devices, own_ref, out_ref, send_sems, recv_sems):
    me = lax.axis_index("ctx")
    barrier = pltpu.get_barrier_semaphore()
    for d in range(1, n_devices):
        pl.semaphore_signal(barrier, inc=1, device_id={"ctx": (me + d) % n_devices})
    pl.semaphore_wait(barrier, n_devices - 1)
    copies = [
        pltpu.make_async_remote_copy(
            src_ref=own_ref,
            dst_ref=out_ref.at[me],
            send_sem=send_sems.at[d],
            recv_sem=recv_sems.at[d],
            device_id={"ctx": (me + d) % n_devices},
        )
        for d in range(1, n_devices)
    ]
    for copy in copies:
        copy.start()
    out_ref[me] = own_ref[...]
    for copy in copies:
        copy.wait()


def gather_rows(own, n_devices):
    vmem = pl.BlockSpec(memory_space=pltpu.VMEM)
    out = pl.pallas_call(
        functools.partial(gather_kernel, n_devices),
        out_shape=jax.ShapeDtypeStruct((n_devices,) + own.shape, own.dtype),
        in_specs=[vmem],
        out_specs=vmem,
        scratch_shapes=[pltpu.SemaphoreType.DMA((n_devices,)), pltpu.SemaphoreType.DMA((n_devices,))],
        compiler_params=pltpu.CompilerParams(collective_id=0, has_side_effects=True),
        name="gather_rows",
    )(own)
    return out.reshape(n_devices * own.shape[0], own.shape[1])


def attend_kernel(
    n_parts, n_chunks, first, width_latent, heads, scale, steps_ref, list_ref, *refs
):
    cache_in = refs[:n_parts]
    q_refs = refs[n_parts : n_parts + n_chunks]
    o_refs = refs[n_parts + n_chunks : n_parts + 2 * n_chunks]
    lse_ref, keys, acc, sems = refs[n_parts + 2 * n_chunks :]
    part_blocks = cache_in[0].shape[0]
    copies = [
        pltpu.make_async_copy(
            cache_in[i], keys.at[pl.ds(i * part_blocks, part_blocks)], sems.at[i]
        )
        for i in range(n_parts)
    ]
    for copy in copies:
        copy.start()
    groups, rows_chunk, _ = o_refs[0].shape
    rows = rows_chunk * n_chunks
    tokens = rows_chunk // heads
    span = STEP * BLK
    token_of_row = (lax.broadcasted_iota(jnp.int32, (rows, 1), 0) // heads) % tokens
    row_bit = lax.shift_left(jnp.ones_like(token_of_row), token_of_row)
    block_of_col = lax.broadcasted_iota(jnp.int32, (1, span), 1) // BLK
    diagonal = lax.broadcasted_iota(jnp.int32, (rows, rows), 0) == lax.broadcasted_iota(
        jnp.int32, (rows, rows), 1
    )
    for copy in copies:
        copy.wait()
    base = 2**tokens

    def one_step(i, g, query, s, peak, total):
        entries = [list_ref[g, s * STEP + k] for k in range(STEP)]
        key_rows = jnp.concatenate([keys[e // base] for e in entries], axis=0)
        bits = jnp.zeros((1, span), jnp.int32)
        for k in range(STEP):
            bits = jnp.where(block_of_col == k, entries[k] % base, bits)
        live = (bits & row_bit) != 0
        scores = (
            lax.dot_general(
                query, key_rows, (((1,), (1,)), ((), ())), preferred_element_type=jnp.float32
            )
            * scale
        )
        scores = jnp.where(live, scores, EMPTY)
        new_peak = jnp.maximum(peak, jnp.max(scores, axis=1, keepdims=True))
        fade = jnp.exp(peak - new_peak)
        exponent = jnp.where(live, jnp.exp(scores - new_peak), 0.0)
        acc[i] = acc[i] * fade + jnp.dot(
            exponent.astype(jnp.bfloat16),
            key_rows[:, :width_latent],
            preferred_element_type=jnp.float32,
        )
        return new_peak, total * fade + jnp.sum(exponent, axis=1, keepdims=True)

    def some_groups(block, carry):
        local_g = [block * SIDE + i for i in range(SIDE)]
        g = [first + x for x in local_g]
        query = [jnp.concatenate([q[x] for q in q_refs], axis=0) for x in g]
        acc[...] = jnp.zeros_like(acc)

        def step(s, states):
            return tuple(
                one_step(i, g[i], query[i], s, *states[i]) for i in range(SIDE)
            )

        start = (jnp.full((rows, 1), EMPTY, jnp.float32), jnp.zeros((rows, 1), jnp.float32))
        n_steps = functools.reduce(jnp.maximum, [steps_ref[x] for x in g])
        states = lax.fori_loop(0, n_steps, step, (start,) * SIDE)
        for i in range(SIDE):
            peak, total = states[i]
            some = total > 0.0
            safe = jnp.where(some, total, 1.0)
            out = (acc[i] / safe).astype(jnp.bfloat16)
            for j in range(n_chunks):
                o_refs[j][local_g[i]] = out[j * rows_chunk : (j + 1) * rows_chunk]
            lse = jnp.where(some, peak + jnp.log(safe), EMPTY)
            lse_ref[pl.ds(local_g[i], 1), :] = jnp.sum(
                jnp.where(diagonal, lse, 0.0), axis=0, keepdims=True
            )
        return carry

    lax.fori_loop(0, groups // SIDE, some_groups, 0)


def attend(parts, chunks, block_list, steps, first, groups, heads, width_latent, scale):
    n_parts, n_chunks = len(parts), len(chunks)
    part_blocks, _, width_row = parts[0].shape
    rows_chunk = chunks[0].shape[1]
    vmem = pl.BlockSpec(memory_space=pltpu.VMEM)
    smem = pl.BlockSpec(memory_space=pltpu.SMEM)
    out = pl.pallas_call(
        functools.partial(attend_kernel, n_parts, n_chunks, first, width_latent, heads, scale),
        out_shape=[jax.ShapeDtypeStruct((groups, rows_chunk, width_latent), jnp.bfloat16)] * n_chunks
        + [jax.ShapeDtypeStruct((groups, rows_chunk * n_chunks), jnp.float32)],
        in_specs=[smem, smem] + [pl.BlockSpec(memory_space=pl.ANY)] * n_parts + [vmem] * n_chunks,
        out_specs=[vmem] * (n_chunks + 1),
        scratch_shapes=[
            pltpu.VMEM((n_parts * part_blocks, BLK, width_row), jnp.bfloat16),
            pltpu.VMEM((SIDE, rows_chunk * n_chunks, width_latent), jnp.float32),
            pltpu.SemaphoreType.DMA((n_parts,)),
        ],
        compiler_params=pltpu.CompilerParams(vmem_limit_bytes=48 * 2**20),
        name="attend",
        cost_estimate=pl.CostEstimate(
            flops=2 * groups * rows_chunk * n_chunks * part_blocks * BLK * (width_row + width_latent),
            bytes_accessed=2 * n_parts * part_blocks * BLK * width_row,
            transcendentals=0,
        ),
    )(steps, block_list, *parts, *chunks)
    return out[:n_chunks], out[n_chunks]


def combine(partials):
    if len(partials) == 1:
        return partials[0]
    logs = [log for _, log in partials]
    top = functools.reduce(jnp.maximum, logs)
    shares = [jnp.exp(x - top) for x in logs]
    total = functools.reduce(jnp.add, shares)
    value = functools.reduce(
        jnp.add,
        [v.astype(jnp.float32) * (s / total)[:, :, None] for (v, _), s in zip(partials, shares)],
    ).astype(jnp.bfloat16)
    return value, top + jnp.log(total)


def project_kernel(bits, tiles, rows_ref, w_ref, out_ref, weights, w_sems, *bufs):
    n_stages = len(bits)
    sends, recvs = bufs[:n_stages], bufs[n_stages : 2 * n_stages]
    send_sems, recv_sems = bufs[2 * n_stages :]
    me = lax.axis_index("ctx")
    upper = [(me // bit) % 2 for bit in bits]
    partner = [me + bit * (1 - 2 * up) for bit, up in zip(bits, upper)]
    width = weights.shape[2]
    loads = [
        pltpu.make_async_copy(
            w_ref.at[:, pl.ds(t * width, width)], weights.at[t], w_sems.at[t]
        )
        for t in range(tiles)
    ]
    for load in loads:
        load.start()
    barrier = pltpu.get_barrier_semaphore()
    for other in partner:
        pl.semaphore_signal(barrier, inc=1, device_id={"ctx": other})
    pl.semaphore_wait(barrier, n_stages)

    def copy_of(k, t):
        return pltpu.make_async_remote_copy(
            src_ref=sends[k].at[t],
            dst_ref=recvs[k].at[t],
            send_sem=send_sems.at[t, k],
            recv_sem=recv_sems.at[t, k],
            device_id={"ctx": partner[k]},
        )

    def send_half(k, t, total):
        half = total.shape[0] // 2
        low, high = total[:half], total[half:]
        sends[k][t] = jnp.where(upper[k] == 1, low, high).astype(jnp.bfloat16)
        copy_of(k, t).start()
        return jnp.where(upper[k] == 1, high, low)

    kept = {}
    for time in range(tiles + n_stages):
        for k in reversed(range(n_stages)):
            t = time - 1 - k
            if 0 <= t < tiles:
                copy_of(k, t).wait()
                total = kept.pop(t) + recvs[k][t].astype(jnp.float32)
                if k + 1 < n_stages:
                    kept[t] = send_half(k + 1, t, total)
                else:
                    out_ref[:, t * width : (t + 1) * width] = total.astype(jnp.bfloat16)
        if time < tiles:
            loads[time].wait()
            total = jnp.dot(rows_ref[...], weights[time], preferred_element_type=jnp.float32)
            kept[time] = send_half(0, time, total)


def project(rows, weight, q_local, n_devices):
    bits = [1 << i for i in range(n_devices.bit_length() - 1)]
    depth, columns = weight.shape
    tiles = max(t for t in range(1, TILES + 1) if columns % (t * 128) == 0)
    width = columns // tiles
    sizes = [rows.shape[0] >> (i + 1) for i in range(len(bits))]
    slots = [pltpu.VMEM((tiles, size, width), jnp.bfloat16) for size in sizes]
    vmem = pl.BlockSpec(memory_space=pltpu.VMEM)
    return pl.pallas_call(
        functools.partial(project_kernel, bits, tiles),
        out_shape=jax.ShapeDtypeStruct((q_local, columns), jnp.bfloat16),
        in_specs=[vmem, pl.BlockSpec(memory_space=pl.ANY)],
        out_specs=vmem,
        scratch_shapes=[
            pltpu.VMEM((tiles, depth, width), jnp.bfloat16),
            pltpu.SemaphoreType.DMA((tiles,)),
            *slots,
            *slots,
            pltpu.SemaphoreType.DMA((tiles, len(bits))),
            pltpu.SemaphoreType.DMA((tiles, len(bits))),
        ],
        compiler_params=pltpu.CompilerParams(
            collective_id=1, has_side_effects=True, vmem_limit_bytes=48 * 2**20
        ),
        name="project",
    )(rows, weight)


def local(
    cache_bits, query_bits, q_latent, q_gain, w_uq, w_uk, w_uv, w_o, latent_cache, kv_scales, selected, counts
):
    n_devices = lax.axis_size("ctx")
    me = lax.axis_index("ctx")
    heads_local, width_content, width_latent = w_uk.shape
    width_row = latent_cache.shape[1]
    width_rotary = width_row - width_latent
    q_local, top_blocks = selected.shape
    blocks_local = latent_cache.shape[0] // BLK
    tiles = kv_scales.shape[1]
    n_parts = 2 ** len(cache_bits)

    cache_t = latent_cache.T
    scaled_t = (
        cache_t[:width_latent].astype(jnp.float32).reshape(tiles, width_latent // tiles, -1)
        * kv_scales.T[:, None, :]
    ).astype(jnp.bfloat16)
    own_cache = (
        jnp.concatenate([scaled_t.reshape(width_latent, -1), cache_t[width_latent:]], axis=0)
        .T.reshape(blocks_local, BLK, width_row)
    )
    latent_f = q_latent.astype(jnp.float32)
    normed = (
        latent_f
        * lax.rsqrt(jnp.mean(latent_f * latent_f, axis=1, keepdims=True) + norm_eps)
        * q_gain
    ).astype(jnp.bfloat16)
    live_sel = jnp.arange(top_blocks, dtype=jnp.int32)[None, :] < counts[:, None]
    owner = jnp.where(live_sel, selected // blocks_local, -1)
    row_width = normed.shape[1] + 2 * top_blocks
    packed = jnp.concatenate(
        [
            normed,
            owner.astype(jnp.bfloat16),
            (selected % blocks_local).astype(jnp.bfloat16),
            jnp.zeros((q_local, -row_width % 128), jnp.bfloat16),
        ],
        axis=1,
    )
    gathered = gather_rows(packed, n_devices)
    gathered, own_cache = lax.optimization_barrier((gathered, own_cache))
    near_bit, far_bit = cache_bits
    far = xor_permute(own_cache, n_devices, far_bit)
    near = xor_permute(own_cache, n_devices, near_bit)
    parts_masks = [0, far_bit, near_bit, far_bit | near_bit]
    row_count = gathered.shape[0]
    latent_width = normed.shape[1]
    all_normed = gathered[:, :latent_width]
    all_owner = gathered[:, latent_width : latent_width + top_blocks].astype(jnp.int32)
    all_inner = gathered[:, latent_width + top_blocks : row_width].astype(jnp.int32)

    projected = jnp.dot(all_normed, w_uq, preferred_element_type=jnp.float32).reshape(
        row_count, heads_local, width_content + width_rotary
    )
    content = projected[:, :, :width_content].astype(jnp.bfloat16)
    positions = jnp.arange(row_count, dtype=jnp.int32).astype(jnp.float32)
    rotated = rotate_rotary(projected[:, :, width_content:], positions).astype(jnp.bfloat16)
    absorbed = jnp.einsum("khn,hnc->khc", content, w_uk, preferred_element_type=jnp.float32).astype(
        jnp.bfloat16
    )
    groups = row_count // q_local
    own_queries = jnp.concatenate([absorbed, rotated], axis=2).reshape(
        groups, q_local * heads_local, width_row
    )
    chunks = [own_queries]
    chunk_masks = [0]
    for bit in reversed(query_bits):
        chunks = chunks + [xor_permute(c, n_devices, bit) for c in chunks]
        chunk_masks = chunk_masks + [m | bit for m in chunk_masks]

    far, chunks[-1] = lax.optimization_barrier((far, chunks[-1]))
    parts = [own_cache, far, near, xor_permute(far, n_devices, near_bit)]

    n_held = n_parts * blocks_local
    place = jnp.full_like(all_owner, -1)
    for i, mask in enumerate(parts_masks):
        place = jnp.where(all_owner == (me ^ mask), i * blocks_local + all_inner, place)
    held = jnp.arange(n_held, dtype=jnp.int32)
    member = jnp.any(
        place.reshape(groups, q_local, top_blocks)[:, :, :, None] == held[None, None, None, :], axis=2
    ).astype(jnp.int32)
    bits = jnp.sum(
        member * lax.shift_left(1, jnp.arange(q_local, dtype=jnp.int32))[None, :, None], axis=1
    )
    needed = (bits > 0).astype(jnp.int32)
    rank = jnp.cumsum(needed, axis=1) - needed
    entry = held[None, :] * 2**q_local + bits
    slot = (rank[:, :, None] == held[None, None, :]) & (needed[:, :, None] == 1)
    block_list = jnp.sum(jnp.where(slot, entry[:, :, None], 0), axis=1)
    steps = (jnp.sum(needed, axis=1) + STEP - 1) // STEP

    scale = 1.0 / math.sqrt(width_content + width_rotary)
    rows_chunk = q_local * heads_local
    groups_call = groups // SPLIT
    halves = []
    for first in range(0, groups, groups_call):
        outs, lse = attend(
            parts, chunks, block_list, steps, first, groups_call, heads_local, width_latent, scale
        )
        held_for = {
            mask: [(outs[i], lse[:, i * rows_chunk : (i + 1) * rows_chunk])]
            for i, mask in enumerate(chunk_masks)
        }
        for bit in query_bits:
            leaving = sorted([m for m in held_for if m & bit], reverse=True)
            going = [combine(held_for.pop(m)) for m in leaving]
            logs = xor_permute(jnp.stack([log for _, log in going]), n_devices, bit)
            for i, mask in enumerate(leaving):
                value = xor_permute(going[i][0], n_devices, bit)
                held_for[mask ^ bit].append((value, logs[i]))
        halves.append(combine(held_for[0])[0])
    latent_out = jnp.concatenate(halves, axis=0)
    head_out = latent_out.reshape(row_count, heads_local, width_latent)
    head_values = jnp.einsum(
        "qhc,hcv->qhv", head_out, w_uv, preferred_element_type=jnp.float32
    ).astype(jnp.bfloat16)
    n_bits = n_devices.bit_length() - 1
    rows = head_values.reshape((2,) * n_bits + (q_local, -1))
    rows = rows.transpose(tuple(reversed(range(n_bits))) + (n_bits, n_bits + 1))
    return project(rows.reshape(row_count, -1), w_o, q_local, n_devices)


def solution(mesh):
    n_devices = mesh.shape["ctx"]
    all_bits = [1 << i for i in range(n_devices.bit_length() - 1)]
    cache_bits, query_bits = all_bits[:2], all_bits[2:]
    in_specs = (
        P(("groups", "ctx"), None),
        P(),
        P(None, "ctx"),
        P("ctx", None, None),
        P("ctx", None, None),
        P("ctx", None),
        P(("groups", "ctx"), None),
        P(("groups", "ctx"), None),
        P(("groups", "ctx"), None),
        P(("groups", "ctx")),
    )
    out_specs = P(("groups", "ctx"), None)
    return jax.shard_map(
        functools.partial(local, cache_bits, query_bits),
        mesh=mesh,
        in_specs=in_specs,
        out_specs=out_specs,
        check_vma=False,
    )
```

```python
import functools
import math

import jax
import jax.numpy as jnp
from jax import lax
from jax.experimental import pallas as pl
from jax.experimental.pallas import tpu as pltpu
from jax.sharding import PartitionSpec as P

BLK = 64
STEP = 8
SIDE = 2
TILES = 7
LAG = 2
PIECES = 2
SPLIT = 1

norm_eps = 1e-06
rope_base = 10000.0
EMPTY = -1e30


def rotate_rotary(rotary, positions):
    half_width = rotary.shape[-1] // 2
    freq_index = jnp.arange(half_width, dtype=jnp.float32)
    inverse_freq = jnp.exp(freq_index * (-2.0 * math.log(rope_base) / rotary.shape[-1]))
    angles = positions[:, None] * inverse_freq[None, :]
    cosine = jnp.cos(angles)[:, None, :]
    sine = jnp.sin(angles)[:, None, :]
    first_half = rotary[:, :, :half_width]
    second_half = rotary[:, :, half_width:]
    return jnp.concatenate(
        [first_half * cosine - second_half * sine, first_half * sine + second_half * cosine], axis=2
    )


def xor_permute(value, n_devices, distance):
    return lax.ppermute(value, "ctx", [(i, i ^ distance) for i in range(n_devices)])


def gather_kernel(n_devices, own_ref, out_ref, send_sems, recv_sems):
    me = lax.axis_index("ctx")
    barrier = pltpu.get_barrier_semaphore()
    for d in range(1, n_devices):
        pl.semaphore_signal(barrier, inc=1, device_id={"ctx": (me + d) % n_devices})
    pl.semaphore_wait(barrier, n_devices - 1)
    copies = [
        pltpu.make_async_remote_copy(
            src_ref=own_ref,
            dst_ref=out_ref.at[me],
            send_sem=send_sems.at[d],
            recv_sem=recv_sems.at[d],
            device_id={"ctx": (me + d) % n_devices},
        )
        for d in range(1, n_devices)
    ]
    for copy in copies:
        copy.start()
    out_ref[me] = own_ref[...]
    for copy in copies:
        copy.wait()


def gather_rows(own, n_devices):
    vmem = pl.BlockSpec(memory_space=pltpu.VMEM)
    out = pl.pallas_call(
        functools.partial(gather_kernel, n_devices),
        out_shape=jax.ShapeDtypeStruct((n_devices,) + own.shape, own.dtype),
        in_specs=[vmem],
        out_specs=vmem,
        scratch_shapes=[pltpu.SemaphoreType.DMA((n_devices,)), pltpu.SemaphoreType.DMA((n_devices,))],
        compiler_params=pltpu.CompilerParams(collective_id=0, has_side_effects=True),
        name="gather_rows",
    )(own)
    return out.reshape(n_devices * own.shape[0], own.shape[1])


def attend_kernel(
    n_parts, n_chunks, first, width_latent, heads, scale, steps_ref, list_ref, *refs
):
    cache_in = refs[:n_parts]
    q_refs = refs[n_parts : n_parts + n_chunks]
    o_refs = refs[n_parts + n_chunks : n_parts + 2 * n_chunks]
    lse_ref, keys, acc, sems = refs[n_parts + 2 * n_chunks :]
    part_blocks = cache_in[0].shape[0]
    copies = [
        pltpu.make_async_copy(
            cache_in[i], keys.at[pl.ds(i * part_blocks, part_blocks)], sems.at[i]
        )
        for i in range(n_parts)
    ]
    for copy in copies:
        copy.start()
    groups, rows_chunk, _ = o_refs[0].shape
    rows = rows_chunk * n_chunks
    tokens = rows_chunk // heads
    span = STEP * BLK
    token_of_row = (lax.broadcasted_iota(jnp.int32, (rows, 1), 0) // heads) % tokens
    row_bit = lax.shift_left(jnp.ones_like(token_of_row), token_of_row)
    block_of_col = lax.broadcasted_iota(jnp.int32, (1, span), 1) // BLK
    diagonal = lax.broadcasted_iota(jnp.int32, (rows, rows), 0) == lax.broadcasted_iota(
        jnp.int32, (rows, rows), 1
    )
    for copy in copies:
        copy.wait()
    base = 2**tokens

    def one_step(i, g, query, s, peak, total):
        entries = [list_ref[g, s * STEP + k] for k in range(STEP)]
        key_rows = jnp.concatenate([keys[e // base] for e in entries], axis=0)
        bits = jnp.zeros((1, span), jnp.int32)
        for k in range(STEP):
            bits = jnp.where(block_of_col == k, entries[k] % base, bits)
        live = (bits & row_bit) != 0
        scores = (
            lax.dot_general(
                query, key_rows, (((1,), (1,)), ((), ())), preferred_element_type=jnp.float32
            )
            * scale
        )
        scores = jnp.where(live, scores, EMPTY)
        new_peak = jnp.maximum(peak, jnp.max(scores, axis=1, keepdims=True))
        fade = jnp.exp(peak - new_peak)
        exponent = jnp.where(live, jnp.exp(scores - new_peak), 0.0)
        acc[i] = acc[i] * fade + jnp.dot(
            exponent.astype(jnp.bfloat16),
            key_rows[:, :width_latent],
            preferred_element_type=jnp.float32,
        )
        return new_peak, total * fade + jnp.sum(exponent, axis=1, keepdims=True)

    def some_groups(block, carry):
        local_g = [block * SIDE + i for i in range(SIDE)]
        g = [first + x for x in local_g]
        query = [jnp.concatenate([q[x] for q in q_refs], axis=0) for x in g]
        acc[...] = jnp.zeros_like(acc)

        def step(s, states):
            return tuple(
                one_step(i, g[i], query[i], s, *states[i]) for i in range(SIDE)
            )

        start = (jnp.full((rows, 1), EMPTY, jnp.float32), jnp.zeros((rows, 1), jnp.float32))
        n_steps = functools.reduce(jnp.maximum, [steps_ref[x] for x in g])
        states = lax.fori_loop(0, n_steps, step, (start,) * SIDE)
        for i in range(SIDE):
            peak, total = states[i]
            some = total > 0.0
            safe = jnp.where(some, total, 1.0)
            out = (acc[i] / safe).astype(jnp.bfloat16)
            for j in range(n_chunks):
                o_refs[j][local_g[i]] = out[j * rows_chunk : (j + 1) * rows_chunk]
            lse = jnp.where(some, peak + jnp.log(safe), EMPTY)
            lse_ref[pl.ds(local_g[i], 1), :] = jnp.sum(
                jnp.where(diagonal, lse, 0.0), axis=0, keepdims=True
            )
        return carry

    lax.fori_loop(0, groups // SIDE, some_groups, 0)


def attend(parts, chunks, block_list, steps, first, groups, heads, width_latent, scale):
    n_parts, n_chunks = len(parts), len(chunks)
    part_blocks, _, width_row = parts[0].shape
    rows_chunk = chunks[0].shape[1]
    vmem = pl.BlockSpec(memory_space=pltpu.VMEM)
    smem = pl.BlockSpec(memory_space=pltpu.SMEM)
    out = pl.pallas_call(
        functools.partial(attend_kernel, n_parts, n_chunks, first, width_latent, heads, scale),
        out_shape=[jax.ShapeDtypeStruct((groups, rows_chunk, width_latent), jnp.bfloat16)] * n_chunks
        + [jax.ShapeDtypeStruct((groups, rows_chunk * n_chunks), jnp.float32)],
        in_specs=[smem, smem] + [pl.BlockSpec(memory_space=pl.ANY)] * n_parts + [vmem] * n_chunks,
        out_specs=[vmem] * (n_chunks + 1),
        scratch_shapes=[
            pltpu.VMEM((n_parts * part_blocks, BLK, width_row), jnp.bfloat16),
            pltpu.VMEM((SIDE, rows_chunk * n_chunks, width_latent), jnp.float32),
            pltpu.SemaphoreType.DMA((n_parts,)),
        ],
        compiler_params=pltpu.CompilerParams(vmem_limit_bytes=48 * 2**20),
        name="attend",
        cost_estimate=pl.CostEstimate(
            flops=2 * groups * rows_chunk * n_chunks * part_blocks * BLK * (width_row + width_latent),
            bytes_accessed=2 * n_parts * part_blocks * BLK * width_row,
            transcendentals=0,
        ),
    )(steps, block_list, *parts, *chunks)
    return out[:n_chunks], out[n_chunks]


def combine(partials):
    if len(partials) == 1:
        return partials[0]
    logs = [log for _, log in partials]
    top = functools.reduce(jnp.maximum, logs)
    shares = [jnp.exp(x - top) for x in logs]
    total = functools.reduce(jnp.add, shares)
    value = functools.reduce(
        jnp.add,
        [v.astype(jnp.float32) * (s / total)[:, :, None] for (v, _), s in zip(partials, shares)],
    ).astype(jnp.bfloat16)
    return value, top + jnp.log(total)


def project_kernel(bits, tiles, rows_ref, w_ref, out_ref, weights, w_sems, *bufs):
    n_stages = len(bits)
    sends, recvs = bufs[:n_stages], bufs[n_stages : 2 * n_stages]
    send_sems, recv_sems = bufs[2 * n_stages :]
    me = lax.axis_index("ctx")
    upper = [(me // bit) % 2 for bit in bits]
    partner = [me + bit * (1 - 2 * up) for bit, up in zip(bits, upper)]
    width = weights.shape[2]
    loads = [
        pltpu.make_async_copy(
            w_ref.at[:, pl.ds(t * width, width)], weights.at[t], w_sems.at[t]
        )
        for t in range(tiles)
    ]
    for load in loads:
        load.start()
    barrier = pltpu.get_barrier_semaphore()
    for other in partner:
        pl.semaphore_signal(barrier, inc=1, device_id={"ctx": other})
    pl.semaphore_wait(barrier, n_stages)

    def copy_of(k, t):
        return pltpu.make_async_remote_copy(
            src_ref=sends[k].at[t],
            dst_ref=recvs[k].at[t],
            send_sem=send_sems.at[t, k],
            recv_sem=recv_sems.at[t, k],
            device_id={"ctx": partner[k]},
        )

    def send_half(k, t, total):
        half = total.shape[0] // 2
        low, high = total[:half], total[half:]
        sends[k][t] = jnp.where(upper[k] == 1, low, high).astype(jnp.bfloat16)
        copy_of(k, t).start()
        return jnp.where(upper[k] == 1, high, low)

    kept = {}
    for time in range(tiles + LAG * n_stages):
        for k in reversed(range(n_stages)):
            t = time - LAG * (k + 1)
            if 0 <= t < tiles:
                copy_of(k, t).wait()
                total = kept.pop(t) + recvs[k][t].astype(jnp.float32)
                if k + 1 < n_stages:
                    kept[t] = send_half(k + 1, t, total)
                else:
                    out_ref[:, t * width : (t + 1) * width] = total.astype(jnp.bfloat16)
        if time < tiles:
            loads[time].wait()
            total = jnp.dot(rows_ref[...], weights[time], preferred_element_type=jnp.float32)
            kept[time] = send_half(0, time, total)


def project(rows, weight, q_local, n_devices):
    bits = [1 << i for i in range(n_devices.bit_length() - 1)]
    depth, columns = weight.shape
    tiles = max(t for t in range(1, TILES + 1) if columns % (t * 128) == 0)
    width = columns // tiles
    sizes = [rows.shape[0] >> (i + 1) for i in range(len(bits))]
    slots = [pltpu.VMEM((tiles, size, width), jnp.bfloat16) for size in sizes]
    vmem = pl.BlockSpec(memory_space=pltpu.VMEM)
    return pl.pallas_call(
        functools.partial(project_kernel, bits, tiles),
        out_shape=jax.ShapeDtypeStruct((q_local, columns), jnp.bfloat16),
        in_specs=[vmem, pl.BlockSpec(memory_space=pl.ANY)],
        out_specs=vmem,
        scratch_shapes=[
            pltpu.VMEM((tiles, depth, width), jnp.bfloat16),
            pltpu.SemaphoreType.DMA((tiles,)),
            *slots,
            *slots,
            pltpu.SemaphoreType.DMA((tiles, len(bits))),
            pltpu.SemaphoreType.DMA((tiles, len(bits))),
        ],
        compiler_params=pltpu.CompilerParams(
            collective_id=1, has_side_effects=True, vmem_limit_bytes=48 * 2**20
        ),
        name="project",
    )(rows, weight)


def local(
    cache_bits, query_bits, q_latent, q_gain, w_uq, w_uk, w_uv, w_o, latent_cache, kv_scales, selected, counts
):
    n_devices = lax.axis_size("ctx")
    me = lax.axis_index("ctx")
    heads_local, width_content, width_latent = w_uk.shape
    width_row = latent_cache.shape[1]
    width_rotary = width_row - width_latent
    q_local, top_blocks = selected.shape
    blocks_local = latent_cache.shape[0] // BLK
    tiles = kv_scales.shape[1]

    cache_t = latent_cache.T
    scaled_t = (
        cache_t[:width_latent].astype(jnp.float32).reshape(tiles, width_latent // tiles, -1)
        * kv_scales.T[:, None, :]
    ).astype(jnp.bfloat16)
    whole_t = jnp.concatenate([scaled_t.reshape(width_latent, -1), cache_t[width_latent:]], axis=0)
    piece_blocks = blocks_local // PIECES
    own_cache = [
        x.T.reshape(piece_blocks, BLK, width_row) for x in jnp.split(whole_t, PIECES, axis=1)
    ]

    latent_f = q_latent.astype(jnp.float32)
    normed = (
        latent_f
        * lax.rsqrt(jnp.mean(latent_f * latent_f, axis=1, keepdims=True) + norm_eps)
        * q_gain
    ).astype(jnp.bfloat16)
    live_sel = jnp.arange(top_blocks, dtype=jnp.int32)[None, :] < counts[:, None]
    owner = jnp.where(live_sel, selected // blocks_local, -1)
    row_width = normed.shape[1] + 2 * top_blocks
    packed = jnp.concatenate(
        [
            normed,
            owner.astype(jnp.bfloat16),
            (selected % blocks_local).astype(jnp.bfloat16),
            jnp.zeros((q_local, -row_width % 128), jnp.bfloat16),
        ],
        axis=1,
    )
    gathered = gather_rows(packed, n_devices)
    gathered, own_cache = lax.optimization_barrier((gathered, own_cache))
    near_bit, far_bit = cache_bits
    far = [xor_permute(x, n_devices, far_bit) for x in own_cache]
    near = [xor_permute(x, n_devices, near_bit) for x in own_cache]
    parts_masks = [0, far_bit, near_bit, far_bit | near_bit]
    row_count = gathered.shape[0]
    latent_width = normed.shape[1]
    all_normed = gathered[:, :latent_width]
    all_owner = gathered[:, latent_width : latent_width + top_blocks].astype(jnp.int32)
    all_inner = gathered[:, latent_width + top_blocks : row_width].astype(jnp.int32)

    projected = jnp.dot(all_normed, w_uq, preferred_element_type=jnp.float32).reshape(
        row_count, heads_local, width_content + width_rotary
    )
    content = projected[:, :, :width_content].astype(jnp.bfloat16)
    positions = jnp.arange(row_count, dtype=jnp.int32).astype(jnp.float32)
    rotated = rotate_rotary(projected[:, :, width_content:], positions).astype(jnp.bfloat16)
    absorbed = jnp.einsum("khn,hnc->khc", content, w_uk, preferred_element_type=jnp.float32).astype(
        jnp.bfloat16
    )
    groups = row_count // q_local
    own_queries = jnp.concatenate([absorbed, rotated], axis=2).reshape(
        groups, q_local * heads_local, width_row
    )
    chunks = [own_queries]
    chunk_masks = [0]
    for bit in reversed(query_bits):
        chunks = chunks + [xor_permute(c, n_devices, bit) for c in chunks]
        chunk_masks = chunk_masks + [m | bit for m in chunk_masks]

    passed = []
    for i, piece in enumerate(far):
        j = len(chunks) - 1 if i + 1 == len(far) else 1
        far[i], chunks[j] = lax.optimization_barrier((piece, chunks[j]))
        passed.append(xor_permute(far[i], n_devices, near_bit))
    parts = own_cache + far + near + passed

    n_held = len(parts) * piece_blocks
    place = jnp.full_like(all_owner, -1)
    for i, mask in enumerate(parts_masks):
        place = jnp.where(all_owner == (me ^ mask), i * blocks_local + all_inner, place)
    held = jnp.arange(n_held, dtype=jnp.int32)
    member = jnp.any(
        place.reshape(groups, q_local, top_blocks)[:, :, :, None] == held[None, None, None, :], axis=2
    ).astype(jnp.int32)
    bits = jnp.sum(
        member * lax.shift_left(1, jnp.arange(q_local, dtype=jnp.int32))[None, :, None], axis=1
    )
    needed = (bits > 0).astype(jnp.int32)
    rank = jnp.cumsum(needed, axis=1) - needed
    entry = held[None, :] * 2**q_local + bits
    slot = (rank[:, :, None] == held[None, None, :]) & (needed[:, :, None] == 1)
    block_list = jnp.sum(jnp.where(slot, entry[:, :, None], 0), axis=1)
    steps = (jnp.sum(needed, axis=1) + STEP - 1) // STEP

    scale = 1.0 / math.sqrt(width_content + width_rotary)
    rows_chunk = q_local * heads_local
    groups_call = groups // SPLIT
    halves = []
    for first in range(0, groups, groups_call):
        outs, lse = attend(
            parts, chunks, block_list, steps, first, groups_call, heads_local, width_latent, scale
        )
        held_for = {
            mask: [(outs[i], lse[:, i * rows_chunk : (i + 1) * rows_chunk])]
            for i, mask in enumerate(chunk_masks)
        }
        for bit in query_bits:
            leaving = sorted([m for m in held_for if m & bit], reverse=True)
            going = [combine(held_for.pop(m)) for m in leaving]
            logs = xor_permute(jnp.stack([log for _, log in going]), n_devices, bit)
            for i, mask in enumerate(leaving):
                value = xor_permute(going[i][0], n_devices, bit)
                held_for[mask ^ bit].append((value, logs[i]))
        halves.append(combine(held_for[0])[0])
    latent_out = jnp.concatenate(halves, axis=0)
    head_out = latent_out.reshape(row_count, heads_local, width_latent)
    head_values = jnp.einsum(
        "qhc,hcv->qhv", head_out, w_uv, preferred_element_type=jnp.float32
    ).astype(jnp.bfloat16)
    n_bits = n_devices.bit_length() - 1
    rows = head_values.reshape((2,) * n_bits + (q_local, -1))
    rows = rows.transpose(tuple(reversed(range(n_bits))) + (n_bits, n_bits + 1))
    return project(rows.reshape(row_count, -1), w_o, q_local, n_devices)


def solution(mesh):
    n_devices = mesh.shape["ctx"]
    all_bits = [1 << i for i in range(n_devices.bit_length() - 1)]
    cache_bits, query_bits = all_bits[:2], all_bits[2:]
    in_specs = (
        P(("groups", "ctx"), None),
        P(),
        P(None, "ctx"),
        P("ctx", None, None),
        P("ctx", None, None),
        P("ctx", None),
        P(("groups", "ctx"), None),
        P(("groups", "ctx"), None),
        P(("groups", "ctx"), None),
        P(("groups", "ctx")),
    )
    out_specs = P(("groups", "ctx"), None)
    return jax.shard_map(
        functools.partial(local, cache_bits, query_bits),
        mesh=mesh,
        in_specs=in_specs,
        out_specs=out_specs,
        check_vma=False,
    )
```
